32 devices in a mesh: member: 2 (over y), lon: 4 (over z), lat: 2 (over x), dp: 2 (over core).
Axes of the slice: x: 2, y: 2, z: 4, core: 2. Of those that a mesh axis runs over, the one named last changes fastest.
Arguments:
- fields: bfloat16 [4, 64, 32, 512], P(('member', 'dp'), 'lat', 'lon'), parts along dimension 0, may hold values from -6 to 6
- cotangent: bfloat16 [4, 64, 32, 512], P(('member', 'dp'), 'lat', 'lon'), parts along dimension 0, may hold values from -6 to 6
- conv_weight: float32 [7, 7, 512], replicated, may hold values from -0.875 to 0.875
- norm_gain: float32 [512], replicated, may hold values from 0.1 to 1.9
- w_qkv: bfloat16 [512, 768], replicated, may hold values from -1 to 1
- w_out: bfloat16 [256, 512], replicated, may hold values from -0.375 to 0.375
Outputs:
- result: bfloat16 [4, 64, 32, 512], P(('member', 'dp'), 'lat', 'lon'), parts along dimension 0
- grad_fields: bfloat16 [4, 64, 32, 512], P(('member', 'dp'), 'lat', 'lon'), parts along dimension 0
- grad_qkv: float32 [1024, 768], P('member'), parts along dimension 0
- grad_out: float32 [512, 512], P('member'), parts along dimension 0
- grad_conv: float32 [14, 7, 512], P('member'), parts along dimension 0
- grad_gain: float32 [1024], P('member'), parts along dimension 0
The draws below stay inside these ranges and needn't reach their ends.
There are 2 independent parts, one for each index of `member`. The reference program is written for one: setup_inputs(seed, part) draws one part's arguments, and reference() takes and returns one part's arrays. A program takes and returns all parts, laid end to end along the dimension named above; an argument that names none is the same for every part. Nothing has to cross between parts.
All inputs are finite; a program needn't handle non-finite values.
Results may differ from the reference program's by a relative error of at most 0.012.
The reference program's roundings to bfloat16 on the way (of `normed`, `projected`, `weights`, `mixed`, `grad_mixed`, `grad_scores` and `grad_projected`) count: a program that leaves them out, or rounds other values in their place, can miss the bound.
Values may be sent and summed in bfloat16 or wider, within the bound.
A program may use at most 64 MiB of HBM per device.

```python
import jax
import jax.numpy as jnp
from jax import lax

D = 512
HEADS = 4
HEAD_DIM = 64
ATT_WIDTH = 256
BATCH = 2
LAT = 64
LON = 32


def draw_w_qkv(key, part):
    base_key = jax.random.fold_in(key, 0)
    deviation = (D // 3) ** (-0.5)
    drawn = jax.random.normal(base_key, (D, 3 * ATT_WIDTH), jnp.float32) * deviation
    drawn = jnp.clip(drawn, -4.0 * deviation, 4.0 * deviation)
    return drawn.astype(jnp.bfloat16)


def steps_of(own_key, shape, cuts, smallest, top_value):
    loudness = 1.0
    for position, shards_of in cuts:
        heights = jax.random.uniform(jax.random.fold_in(jax.random.fold_in(own_key, 6), position), (shards_of,), jnp.float32, smallest / len(cuts), top_value / len(cuts))
        loudness = loudness * jnp.repeat(jnp.exp(heights), shape[position] // shards_of).reshape((-1,) + (1,) * (len(shape) - 1 - position))
    return loudness


def bell_draw(own_key, extent, scale, bound, cuts=(), kind=jnp.bfloat16):
    factor_of = steps_of(own_key, extent, cuts, -0.22, 0.18) if cuts else 1.0
    drawn = jax.random.normal(own_key, extent, jnp.float32) * scale * factor_of
    return jnp.minimum(jnp.maximum(drawn, -bound), bound).astype(kind)


def setup_inputs(seed: int = 0, part: int = 0) -> dict:
    streams_of = jax.random.split(jax.random.key(seed), 7)
    part_keys = jax.random.split(jax.random.fold_in(streams_of[6], part), 7)
    return {
        "fields": bell_draw(part_keys[0], (BATCH, LAT, LON, D), 1.0, 6.0, ((0, 2), (1, 2), (2, 4))),
        "cotangent": bell_draw(part_keys[1], (BATCH, LAT, LON, D), 1.0, 6.0, ((0, 2), (1, 2), (2, 4))),
        "conv_weight": bell_draw(streams_of[2], (7, 7, D), 49 ** -0.5, 0.875, (), jnp.float32),
        "norm_gain": jnp.clip(1.0 + 0.18 * jax.random.normal(streams_of[3], (D,), jnp.float32), 0.1, 1.9),
        "w_qkv": draw_w_qkv(jax.random.fold_in(streams_of[6], 71), part),
        "w_out": bell_draw(streams_of[5], (ATT_WIDTH, D), ATT_WIDTH ** -0.5, 0.375),
    }


EPSILON = 1e-06

def wrap_pad(values):
    padded = jnp.pad(values, ((3, 3), (0, 0), (0, 0)))
    return jnp.concatenate([padded[:, -3:], padded, padded[:, :3]], axis=1)

def spread(padded, kernel, lat_rows, lon_cols):
    summed = jnp.zeros((lat_rows, lon_cols, padded.shape[2]), jnp.float32)
    for row_shift in range(7):
        for col_shift in range(7):
            window = padded[row_shift:row_shift + lat_rows, col_shift:col_shift + lon_cols]
            summed = summed + kernel[row_shift, col_shift] * window
    return summed

def correlate(padded, upstream, lat_rows, lon_cols):
    pieces = []
    for row_shift in range(7):
        for col_shift in range(7):
            window = padded[row_shift:row_shift + lat_rows, col_shift:col_shift + lon_cols]
            pieces.append(lax.optimization_barrier(jnp.sum(window * upstream, axis=(0, 1))))
    return jnp.stack(pieces).reshape(7, 7, -1)

def split_heads(values):
    return values.reshape(values.shape[:-1] + (HEADS, HEAD_DIM)).astype(jnp.float32)

def attend_forward(projected):
    queries = split_heads(projected[..., :ATT_WIDTH])
    keys_part = split_heads(projected[..., ATT_WIDTH:2 * ATT_WIDTH])
    values_part = split_heads(projected[..., 2 * ATT_WIDTH:])
    scores = jnp.einsum('...qhd,...khd->...hqk', queries, keys_part) * HEAD_DIM ** (-0.5)
    probs = jax.nn.softmax(scores, axis=-1)
    weights = lax.optimization_barrier(probs.astype(jnp.bfloat16)).astype(jnp.float32)
    mixed = jnp.einsum('...hqk,...khd->...qhd', weights, values_part)
    return (mixed.reshape(projected.shape[:-1] + (ATT_WIDTH,)).astype(jnp.bfloat16), probs)

def attend_backward(projected, probs, grad_mixed):
    queries = split_heads(projected[..., :ATT_WIDTH])
    keys_part = split_heads(projected[..., ATT_WIDTH:2 * ATT_WIDTH])
    values_part = split_heads(projected[..., 2 * ATT_WIDTH:])
    grad_heads = split_heads(grad_mixed)
    weights = lax.optimization_barrier(probs.astype(jnp.bfloat16)).astype(jnp.float32)
    grad_probs = jnp.einsum('...qhd,...khd->...hqk', grad_heads, values_part)
    inner = lax.optimization_barrier(jnp.sum(probs * grad_probs, -1, keepdims=True))
    grad_scores = (probs * (grad_probs - inner) * HEAD_DIM ** (-0.5)).astype(jnp.bfloat16)
    grad_scores = lax.optimization_barrier(grad_scores).astype(jnp.float32)
    grad_query = jnp.einsum('...hqk,...khd->...qhd', grad_scores, keys_part)
    grad_key = jnp.einsum('...hqk,...qhd->...khd', grad_scores, queries)
    grad_value = jnp.einsum('...hqk,...qhd->...khd', weights, grad_heads)
    shaped = projected.shape[:-1] + (ATT_WIDTH,)
    return jnp.concatenate([grad_query.reshape(shaped).astype(jnp.bfloat16), grad_key.reshape(shaped).astype(jnp.bfloat16), grad_value.reshape(shaped).astype(jnp.bfloat16)], axis=-1)

def reference(fields, cotangent, conv_weight, norm_gain, w_qkv, w_out):

    def single_sample(paired):
        sample, upstream = paired
        sample_float = sample.astype(jnp.float32)
        padded = wrap_pad(sample_float)
        update = sample_float + spread(padded, conv_weight, LAT, LON)
        inverse = lax.rsqrt(lax.optimization_barrier(jnp.mean(update * update, -1, keepdims=True)) + EPSILON)
        normed = (update * inverse * norm_gain).astype(jnp.bfloat16)
        normed_flat = normed.reshape(LAT * LON, D)
        projected = jnp.dot(normed_flat, w_qkv, preferred_element_type=jnp.float32).astype(jnp.bfloat16)
        projected = projected.reshape(LAT, LON, 3 * ATT_WIDTH)
        mixed, probs = attend_forward(projected)
        mixed_flat = mixed.reshape(LAT * LON, ATT_WIDTH)
        result = (update + jnp.dot(mixed_flat, w_out, preferred_element_type=jnp.float32).reshape(LAT, LON, D)).astype(jnp.bfloat16)
        upstream_flat = upstream.reshape(LAT * LON, D)
        grad_mixed = jnp.dot(upstream_flat, w_out.T, preferred_element_type=jnp.float32).astype(jnp.bfloat16)
        grad_out = jnp.dot(mixed_flat.T, upstream_flat, preferred_element_type=jnp.float32)
        grad_projected = attend_backward(projected, probs, grad_mixed.reshape(LAT, LON, ATT_WIDTH))
        grad_flat = grad_projected.reshape(LAT * LON, 3 * ATT_WIDTH)
        grad_weight = jnp.dot(normed_flat.T, grad_flat, preferred_element_type=jnp.float32)
        grad_normed = jnp.dot(grad_flat, w_qkv.T, preferred_element_type=jnp.float32).reshape(LAT, LON, D)
        grad_gain = lax.optimization_barrier(jnp.sum(grad_normed * (update * inverse), axis=(0, 1)))
        gained = norm_gain * grad_normed
        grad_update = upstream.astype(jnp.float32) + inverse * gained - update * inverse ** 3 * lax.optimization_barrier(jnp.mean(gained * update, -1, keepdims=True))
        grad_sample = (grad_update + spread(wrap_pad(grad_update), conv_weight[::-1, ::-1], LAT, LON)).astype(jnp.bfloat16)
        grad_conv = correlate(padded, grad_update, LAT, LON)
        return (result, grad_sample, grad_weight, grad_out, grad_conv, grad_gain)
    outputs = lax.map(single_sample, (fields, cotangent))
    return (outputs[0], outputs[1], lax.optimization_barrier(jnp.sum(outputs[2], 0)), lax.optimization_barrier(jnp.sum(outputs[3], 0)), lax.optimization_barrier(jnp.sum(outputs[4], 0)), lax.optimization_barrier(jnp.sum(outputs[5], 0)))
```

```python
import functools
import itertools

import jax
import jax.numpy as jnp
from jax import lax
from jax.experimental import pallas as pl
from jax.experimental.pallas import tpu as pltpu
from jax.sharding import PartitionSpec as P

HEADS = 4
HEAD_DIM = 64


EPSILON = 1e-06


def with_halo(x, sides, width, wrap):
    for axis, dim in sides:
        size, length = (lax.axis_size(axis), x.shape[dim])
        up = [(i, (i + 1) % size) for i in range(size if wrap else size - 1)]
        down = [(j, i) for i, j in up]
        last = lax.slice_in_dim(x, length - width, length, axis=dim)
        first = lax.slice_in_dim(x, 0, width, axis=dim)
        before = lax.ppermute(last, axis, up)
        after = lax.ppermute(first, axis, down)
        x = jnp.concatenate([before, x, after], axis=dim)
    return x


def spread(padded, kernel, lat_rows, lon_cols):
    summed = jnp.zeros(padded.shape[:1] + (lat_rows, lon_cols, padded.shape[3]), jnp.float32)
    for row_shift in range(7):
        band = padded[:, row_shift : row_shift + lat_rows].astype(jnp.float32)
        partial_row = kernel[row_shift, 0] * band[:, :, 0:lon_cols]
        for col_shift in range(1, 7):
            partial_row = (
                partial_row
                + kernel[row_shift, col_shift] * band[:, :, col_shift : col_shift + lon_cols]
            )
        summed = summed + partial_row
    return summed


def correlate(padded, upstream, lat_rows, lon_cols):
    pieces = []
    for row_shift in range(7):
        for col_shift in range(7):
            window = padded[
                :, row_shift : row_shift + lat_rows, col_shift : col_shift + lon_cols
            ].astype(jnp.float32)
            pieces.append(jnp.sum(window * upstream, axis=(0, 1, 2)))
    return jnp.stack(pieces).reshape(7, 7, -1)


def split_heads(values):
    return values.reshape(values.shape[:-1] + (HEADS, HEAD_DIM))


def attend_forward(rowwise, att_width):
    queries = split_heads(rowwise[..., :att_width])
    keys_part = split_heads(rowwise[..., att_width : 2 * att_width])
    values_part = split_heads(rowwise[..., 2 * att_width :])
    scores = jnp.einsum(
        "brqhd,brkhd->brhqk", queries, keys_part, preferred_element_type=jnp.float32
    ) * HEAD_DIM ** (-0.5)
    row_peak = jnp.max(scores, -1, keepdims=True)
    raised = jnp.exp(scores - row_peak)
    probs = raised / jnp.sum(raised, -1, keepdims=True)
    weights = probs.astype(jnp.bfloat16)
    mixed = jnp.einsum(
        "brhqk,brkhd->brqhd", weights, values_part, preferred_element_type=jnp.float32
    )
    return (mixed.reshape(rowwise.shape[:3] + (att_width,)).astype(jnp.bfloat16), probs)


def attend_backward(rowwise, probs, grad_rowwise, att_width):
    queries = split_heads(rowwise[..., :att_width])
    keys_part = split_heads(rowwise[..., att_width : 2 * att_width])
    values_part = split_heads(rowwise[..., 2 * att_width :])
    grad_heads = split_heads(grad_rowwise)
    weights = probs.astype(jnp.bfloat16)
    grad_probs = jnp.einsum(
        "brqhd,brkhd->brhqk", grad_heads, values_part, preferred_element_type=jnp.float32
    )
    inner = jnp.sum(probs * grad_probs, -1, keepdims=True)
    grad_scores = (probs * (grad_probs - inner) * HEAD_DIM ** (-0.5)).astype(jnp.bfloat16)
    grad_query = jnp.einsum(
        "brhqk,brkhd->brqhd", grad_scores, keys_part, preferred_element_type=jnp.float32
    )
    grad_key = jnp.einsum(
        "brhqk,brqhd->brkhd", grad_scores, queries, preferred_element_type=jnp.float32
    )
    grad_value = jnp.einsum(
        "brhqk,brqhd->brkhd", weights, grad_heads, preferred_element_type=jnp.float32
    )
    shaped = rowwise.shape[:3] + (att_width,)
    return jnp.concatenate(
        [
            grad_query.reshape(shaped).astype(jnp.bfloat16),
            grad_key.reshape(shaped).astype(jnp.bfloat16),
            grad_value.reshape(shaped).astype(jnp.bfloat16),
        ],
        axis=-1,
    )


def contract_rows(left, right):
    return lax.dot_general(
        left, right, (((0,), (0,)), ((), ())), preferred_element_type=jnp.float32
    )


def contract_cols(left, right):
    return lax.dot_general(
        left, right, (((1,), (1,)), ((), ())), preferred_element_type=jnp.float32
    )


def on_device_native(fields, cotangent, conv_weight, norm_gain, w_qkv, w_out):
    batch_count, lat_rows, lon_cols, channels = fields.shape
    att_width = w_out.shape[0]
    wide = with_halo(fields, (("lon", 2),), 3, True)
    padded = with_halo(wide, (("lat", 1),), 3, False)
    update = fields.astype(jnp.float32) + spread(padded, conv_weight, lat_rows, lon_cols)
    inverse = lax.rsqrt(jnp.mean(update * update, -1, keepdims=True) + EPSILON)
    normed = (update * inverse * norm_gain).astype(jnp.bfloat16)
    normed_flat = normed.reshape(-1, channels)
    projected = jnp.dot(normed_flat, w_qkv, preferred_element_type=jnp.float32).astype(jnp.bfloat16)
    rowwise = lax.all_to_all(
        projected.reshape(batch_count, lat_rows, lon_cols, 3 * att_width),
        "lon",
        split_axis=1,
        concat_axis=2,
        tiled=True,
    )
    mixed_rows, probs = attend_forward(rowwise, att_width)
    mixed = lax.all_to_all(mixed_rows, "lon", split_axis=2, concat_axis=1, tiled=True)
    mixed_flat = mixed.reshape(-1, att_width)
    result = (
        update
        + jnp.dot(mixed_flat, w_out, preferred_element_type=jnp.float32).reshape(update.shape)
    ).astype(jnp.bfloat16)
    upstream_flat = cotangent.reshape(-1, channels)
    grad_mixed = contract_cols(upstream_flat, w_out).astype(jnp.bfloat16)
    grad_out = contract_rows(mixed_flat, upstream_flat)
    grad_rowwise = lax.all_to_all(
        grad_mixed.reshape(batch_count, lat_rows, lon_cols, att_width),
        "lon",
        split_axis=1,
        concat_axis=2,
        tiled=True,
    )
    grad_projected_rows = attend_backward(rowwise, probs, grad_rowwise, att_width)
    grad_projected = lax.all_to_all(
        grad_projected_rows, "lon", split_axis=2, concat_axis=1, tiled=True
    )
    grad_flat = grad_projected.reshape(-1, 3 * att_width)
    grad_weight = contract_rows(normed_flat, grad_flat)
    grad_normed = contract_cols(grad_flat, w_qkv).reshape(update.shape)
    grad_gain = jnp.sum(grad_normed * (update * inverse), axis=(0, 1, 2))
    gained = norm_gain * grad_normed
    grad_update = (
        cotangent.astype(jnp.float32)
        + inverse * gained
        - update * inverse**3 * jnp.mean(gained * update, -1, keepdims=True)
    )
    grad_wide = with_halo(grad_update.astype(jnp.bfloat16), (("lon", 2),), 3, True).astype(
        grad_update.dtype
    )
    grad_padded = with_halo(grad_wide.astype(jnp.bfloat16), (("lat", 1),), 3, False).astype(
        grad_wide.dtype
    )
    grad_fields = (
        grad_update + spread(grad_padded, conv_weight[::-1, ::-1], lat_rows, lon_cols)
    ).astype(jnp.bfloat16)
    grad_conv = correlate(padded, grad_update, lat_rows, lon_cols)
    totals = lax.psum((grad_weight, grad_out, grad_conv, grad_gain), ("lon", "lat", "dp"))
    return (result, grad_fields, totals[0], totals[1], totals[2], totals[3])


MESH = pl.DeviceIdType.MESH
AXES = ("lat", "lon", "dp")
LANES = 128


def place():
    return tuple(lax.axis_index(a) for a in AXES)


def greet(sizes):
    me = place()
    barrier = pltpu.get_barrier_semaphore()
    count = 0
    for offset in itertools.product(*(range(s) for s in sizes)):
        if not any(offset):
            continue
        target = {a: lax.rem(m + o, s) for a, m, o, s in zip(AXES, me, offset, sizes)}
        pl.semaphore_signal(barrier, inc=1, device_id=target, device_id_type=MESH)
        count += 1
    pl.semaphore_wait(barrier, count)


def remote(src, dst, send, recv, target):
    return pltpu.make_async_remote_copy(
        src_ref=src, dst_ref=dst, send_sem=send, recv_sem=recv, device_id=target, device_id_type=MESH
    )


def roles(own):
    lat, lon, dp = place()
    side = lon // 2
    spot = 2 * lax.rem(lon, 2) + dp

    def block(p):
        return p + lat * (3 - 2 * p)

    def owner(p):
        return {"lon": 2 * dp + p // 2, "dp": p % 2}

    def mine(p):
        return (lon == 2 * dp + p // 2) & (dp == p % 2)

    def source(i):
        return {"lon": i, "dp": side}

    def local(i):
        return (lon == i) & (dp == side)

    def rows(p):
        return pl.ds(own * block(p), own)

    return lon, spot, owner, mine, source, local, rows


def take_rows(own, src, dst, send, recv, stay):
    lon, _, owner, mine, source, local, rows = roles(own)

    def there(p):
        return remote(src.at[rows(p)], dst.at[:, lon], send.at[p], recv.at[lon], owner(p))

    def here(p, i):
        return pltpu.make_async_copy(src.at[rows(p)], dst.at[:, i], stay)

    def start():
        for p in range(4):

            @pl.when(jnp.logical_not(mine(p)))
            def _(p=p):
                there(p).start()

            @pl.when(mine(p))
            def _(p=p):
                here(p, lon).start()

    def wait():
        for i in range(4):

            @pl.when(local(i))
            def _(i=i):
                here(0, i).wait()

            @pl.when(jnp.logical_not(local(i)))
            def _(i=i):
                remote(src.at[rows(0)], dst.at[:, i], send.at[0], recv.at[i], source(i)).wait_recv()

    def wait_sent():
        for p in range(4):

            @pl.when(jnp.logical_not(mine(p)))
            def _(p=p):
                there(p).wait_send()

    return start, wait, wait_sent


def give_rows(own, src, dst, send, recv, stay):
    lon, spot, owner, mine, source, local, rows = roles(own)

    def there(i):
        return remote(src.at[:, i], dst.at[rows(spot)], send.at[i], recv.at[spot], source(i))

    def here(i):
        return pltpu.make_async_copy(src.at[:, i], dst.at[rows(spot)], stay)

    def start():
        for i in range(4):

            @pl.when(jnp.logical_not(local(i)))
            def _(i=i):
                there(i).start()

            @pl.when(local(i))
            def _(i=i):
                here(i).start()

    def wait():
        for p in range(4):

            @pl.when(jnp.logical_not(mine(p)))
            def _(p=p):
                remote(src.at[:, 0], dst.at[rows(p)], send.at[0], recv.at[p], owner(p)).wait_recv()

        for i in range(4):

            @pl.when(jnp.logical_not(local(i)))
            def _(i=i):
                there(i).wait_send()

            @pl.when(local(i))
            def _(i=i):
                here(i).wait()

    return start, wait


def halo_rows(first, last, top, low, send, recv):
    lat, lon, dp = place()
    side = lon // 2
    spot = 2 * lax.rem(lon, 2) + dp
    index, end = 4 * lat + spot + lat * (3 - 2 * spot), 7

    def at(k):
        k = lax.rem(k + 8, 8)
        band = k // 4
        b = lax.rem(k, 4)
        p = b + band * (3 - 2 * b)
        return {"lat": band, "lon": 2 * side + p // 2, "dp": lax.rem(p, 2)}

    down = remote(last, top, send.at[0], recv.at[0], at(index + 1))
    up = remote(first, low, send.at[1], recv.at[1], at(index + 7))

    def start():
        @pl.when(index < end)
        def _():
            down.start()

        @pl.when(index > 0)
        def _():
            up.start()

        @pl.when(index == 0)
        def _():
            top[...] = jnp.zeros(top.shape, top.dtype)

        @pl.when(index == end)
        def _():
            low[...] = jnp.zeros(low.shape, low.dtype)

    def wait():
        @pl.when(index > 0)
        def _():
            down.wait_recv()
            up.wait_send()

        @pl.when(index < end)
        def _():
            up.wait_recv()
            down.wait_send()

    return start, wait


def convolve(pad, weight, out, own, flip, halo):
    circle, channels = pad.shape[1], pad.shape[2]
    taken = {}
    for r in range(own):
        taps = [a for a in range(7) if (3 <= r + a < own + 3) != halo]
        if taps:
            taken[r] = taps

    def chunk(c, carry):
        lanes = pl.ds(pl.multiple_of(c * LANES, LANES), LANES)
        totals = {r: out[r, :, lanes] if halo else pad[r + 3, :, lanes] for r in taken}
        for e in range(7):
            turn = (3 - e) % circle
            column = 6 - e if flip else e
            taps = [weight[6 - a if flip else a, column : column + 1, lanes] for a in range(7)]
            for r in taken:
                part = None
                for a in taken[r]:
                    term = pad[r + a, :, lanes] * taps[a]
                    part = term if part is None else part + term
                if turn:
                    part = pltpu.roll(part, turn, 0)
                totals[r] = totals[r] + part
        for r in taken:
            out[r, :, lanes] = totals[r]
        return carry

    lax.fori_loop(0, channels // LANES, chunk, 0)


def correlate_rows(pad, upstream, out, own, low, high):
    circle = pad.shape[1]

    def chunk(c, carry):
        lanes = pl.ds(pl.multiple_of(c * LANES, LANES), LANES)
        for e in range(7):
            turn = (e - 3) % circle
            turned = [upstream[r, :, lanes] for r in range(own)]
            if turn:
                turned = [pltpu.roll(t, turn, 0) for t in turned]
            for a in range(7):
                total = None
                for r in range(own):
                    term = pad[r + a, :, lanes] * turned[r]
                    total = term if total is None else total + term
                out[a, e : e + 1, lanes] = jnp.sum(total, axis=0, keepdims=True)
        return carry

    lax.fori_loop(low, high, chunk, 0)


def dot(left, right, dims):
    return lax.dot_general(left, right, (dims, ((), ())), preferred_element_type=jnp.float32)


PLAIN, COLS, ROWS = ((1,), (0,)), ((1,), (1,)), ((0,), (0,))


def attend_rows(projected, circle, att_width):
    cells = projected.shape[0]
    group = max(circle, LANES)
    row_of = lax.broadcasted_iota(jnp.int32, (group, group), 0) // circle
    col_of = lax.broadcasted_iota(jnp.int32, (group, group), 1) // circle
    same = row_of == col_of
    lane_head = lax.broadcasted_iota(jnp.int32, (group, LANES), 1) // HEAD_DIM
    bf16 = jnp.bfloat16
    zero = jnp.zeros((), bf16)
    heads = range(LANES // HEAD_DIM)
    groups = [slice(g * group, (g + 1) * group) for g in range(cells // group)]
    pairs = [slice(p * LANES, (p + 1) * LANES) for p in range(att_width // LANES)]

    def third(k, cut, at):
        return projected[cut, k * att_width : (k + 1) * att_width][:, at]

    def join(parts):
        whole = parts[0]
        for h in heads[1:]:
            whole = jnp.where(lane_head == h, parts[h], whole)
        return whole.astype(bf16)

    kept, mixed = {}, []
    for g, cut in enumerate(groups):
        found = []
        for p, at in enumerate(pairs):
            q, k, v = (third(n, cut, at) for n in range(3))
            parts = []
            for h in heads:
                scores = dot(jnp.where(lane_head == h, q, zero), k, COLS) * HEAD_DIM ** (-0.5)
                scores = jnp.where(same, scores, -jnp.inf)
                raised = jnp.exp(scores - jnp.max(scores, -1, keepdims=True))
                probs = raised / jnp.sum(raised, -1, keepdims=True)
                kept[g, p, h] = probs
                parts.append(dot(probs.astype(bf16), v, PLAIN))
            found.append(join(parts))
        mixed.append(jnp.concatenate(found, axis=1))

    def backward(grad_mixed):
        grads = []
        for g, cut in enumerate(groups):
            found = [[], [], []]
            for p, at in enumerate(pairs):
                q, k, v = (third(n, cut, at) for n in range(3))
                up = grad_mixed[cut, at]
                parts = [[], [], []]
                for h in heads:
                    probs = kept[g, p, h]
                    grad_probs = dot(jnp.where(lane_head == h, up, zero), v, COLS)
                    inner = jnp.sum(probs * grad_probs, -1, keepdims=True)
                    grad_scores = (probs * (grad_probs - inner) * HEAD_DIM ** (-0.5)).astype(bf16)
                    parts[0].append(dot(grad_scores, k, PLAIN))
                    parts[1].append(dot(grad_scores, q, ROWS))
                    parts[2].append(dot(probs.astype(bf16), up, ROWS))
                for part, into in zip(parts, found):
                    into.append(join(part))
            grads.append(jnp.concatenate(found[0] + found[1] + found[2], axis=1))
        return jnp.concatenate(grads, axis=0)

    return jnp.concatenate(mixed, axis=0), backward


def core_step(cr_ref, update_ref, gain, wq_ref, wo_ref, result_ref, gu_ref, gub_ref, bq_refs, bo_ref, gg_ref):
    own, blocks, width, channels = cr_ref.shape
    circle, cells = blocks * width, own * blocks * width
    att_width = wo_ref.shape[0]
    bf16 = jnp.bfloat16
    update = update_ref[...].reshape(cells, channels)
    inverse = lax.rsqrt(jnp.mean(update * update, -1, keepdims=True) + EPSILON)
    normed = (update * inverse * gain).astype(bf16)
    projected = dot(normed, wq_ref[...], PLAIN).astype(bf16)
    mixed, backward = attend_rows(projected, circle, att_width)
    result = update + dot(mixed, wo_ref[...], PLAIN)
    result_ref[...] = result.reshape(result_ref.shape).astype(bf16)
    yield
    cot32 = cr_ref[...].astype(jnp.float32).reshape(cells, channels)
    cot = cot32.astype(bf16)
    bo_ref[...] = dot(mixed, cot, ROWS).astype(bf16).reshape(bo_ref.shape)
    yield
    grad_mixed = dot(cot, wo_ref[...], COLS).astype(bf16)
    grad_projected = backward(grad_mixed)
    grad_normed = dot(grad_projected, wq_ref[...], COLS)
    gained = gain * grad_normed
    grad_update = (
        cot32
        + inverse * gained
        - update * (inverse * inverse * inverse) * jnp.mean(gained * update, -1, keepdims=True)
    )
    gu_ref[...] = grad_update.reshape(gu_ref.shape)
    gub_ref[...] = grad_update.reshape(gub_ref.shape).astype(bf16)
    yield
    for k, ref in enumerate(bq_refs):
        part = ref.shape[2]
        piece = dot(normed, grad_projected[:, k * part : (k + 1) * part], ROWS)
        ref[...] = piece.astype(bf16).reshape(ref.shape)
    yield
    gg_ref[...] = jnp.sum(grad_normed * (update * inverse), axis=0, keepdims=True)
    yield


def pack_small(big, conv, gg_ref):
    channels = gg_ref.shape[1]
    fill = big.shape[0] * big.shape[1] - 50
    small = jnp.concatenate(
        [conv[a] for a in range(7)] + [gg_ref[...], jnp.zeros((fill, channels), jnp.float32)], axis=0
    )
    big[...] = small.astype(jnp.bfloat16).reshape(big.shape)


def finish(*refs):
    every, outs = refs[: len(refs) - 6], refs[len(refs) - 6 :]
    result_ref, gf_ref, out_ref, small_ref = every[:4]
    result_out, gf_out, gq_out, go_out, gc_out, gg_out = outs
    f32 = jnp.float32
    result_out[...] = result_ref[...]
    gf_out[...] = gf_ref[...]
    for k, ref in enumerate(every[4:]):
        part = ref.shape[2]
        gq_out[:, k * part : (k + 1) * part] = ref[...].astype(f32).reshape(gq_out.shape[0], part)
    go_out[...] = out_ref[...].astype(f32).reshape(go_out.shape)
    small = small_ref[...].astype(f32).reshape(-1, go_out.shape[1])
    for a in range(7):
        gc_out[a] = small[a * 7 : (a + 1) * 7]
    gg_out[...] = small[49:50]


def sum_stages(big, every, got1, sum1, got2, sum2, got3, sum3, got4, send, recv):
    lat, lon, dp = place()
    f32 = jnp.float32
    other_dp, other_lat = 1 - dp, 1 - lat
    half = lon // 2
    inner = (lon == 1) | (lon == 2)
    outer = jnp.logical_not(inner)
    mine, across = every.at[2 * dp + lat], every.at[2 * dp + other_lat]
    core = remote(big.at[pl.ds(2 * other_dp, 2)], got1, send.at[0], recv.at[0], {"dp": other_dp})
    band = remote(sum1.at[other_lat], got2, send.at[1], recv.at[1], {"lat": other_lat})
    inward = remote(sum2, got3, send.at[2], recv.at[2], {"lon": 1 + half})
    middle = remote(sum3, got4, send.at[3], recv.at[3], {"lon": 3 - lon})
    out_band = remote(mine, mine, send.at[4], recv.at[4], {"lat": other_lat})
    out_lon = remote(mine, mine, send.at[5], recv.at[5], {"lon": 3 * half})
    out_both = remote(mine, mine, send.at[6], recv.at[6], {"lat": other_lat, "lon": 3 * half})
    in_band = remote(across, across, send.at[4], recv.at[4], {"lat": other_lat})
    in_both = remote(across, across, send.at[6], recv.at[6], {"lat": other_lat, "lon": 1 + half})
    ours, theirs = every.at[pl.ds(2 * dp, 2)], every.at[pl.ds(2 * other_dp, 2)]
    out_core = remote(ours, ours, send.at[7], recv.at[7], {"dp": other_dp})
    in_core = remote(theirs, theirs, send.at[7], recv.at[7], {"dp": other_dp})

    def add(a, b, to):
        to[...] = (a[...].astype(f32) + b[...].astype(f32)).astype(to.dtype)

    def s0():
        core.start()

    def s1():
        core.wait()
        add(big.at[pl.ds(2 * dp, 2)], got1, sum1)
        band.start()

    def s2():
        band.wait()
        add(sum1.at[lat], got2, sum2)

        @pl.when(outer)
        def _():
            inward.start()

    def s3():
        @pl.when(inner)
        def _():
            inward.wait_recv()
            add(sum2, got3, sum3)
            middle.start()

    def s4():
        @pl.when(inner)
        def _():
            middle.wait()
            add(sum3, got4, mine)
            out_lon.start()
            out_both.start()
            out_band.start()

    def s5():
        @pl.when(inner)
        def _():
            in_band.wait_recv()
            out_core.start()

        @pl.when(outer)
        def _():
            out_lon.wait_recv()
            in_both.wait_recv()
            out_core.start()

    def s6():
        out_core.wait_send()
        in_core.wait_recv()

        @pl.when(inner)
        def _():
            out_lon.wait_send()
            out_both.wait_send()
            out_band.wait_send()

        @pl.when(outer)
        def _():
            inward.wait_send()

    return s0, s1, s2, s3, s4, s5, s6


def layer(sizes, f_ref, c_ref, w_hbm, gain_ref, wq_hbm, wo_hbm, result_out, gf_out, *rest):
    every, rest = rest[:STREAMS], rest[STREAMS:]
    (fp, cr, weight, wq, wo, pad, update, result, gpad, gub, gg, low, out, gf, conv,
     f_send, f_recv, c_send, c_recv, stay, fh_send, fh_recv, gh_send, gh_recv,
     r_send, r_recv, g_send, g_recv), rest = rest[:28], rest[28:]
    own, circle, channels = update.shape
    f32, bf16 = jnp.float32, jnp.bfloat16
    loads = [
        pltpu.make_async_copy(src, dst, stay.at[k])
        for k, (src, dst) in enumerate(((w_hbm, weight), (wq_hbm, wq), (wo_hbm, wo)))
    ]
    for load in loads:
        load.start()
    per = len(rest) // STREAMS
    bigs = [rest[k * per] for k in range(STREAMS)]
    streams = [sum_stages(bigs[k], every[k], *rest[k * per + 1 : (k + 1) * per - 2], *rest[(k + 1) * per - 2 : (k + 1) * per])
               for k in range(STREAMS)]
    head, small, body = streams[0], streams[1], streams[2:]
    start_f, wait_f, sent_f = take_rows(own, f_ref, fp.at[pl.ds(3, own)], f_send, f_recv, stay.at[3])
    start_c, wait_c, sent_c = take_rows(own, c_ref, cr, c_send, c_recv, stay.at[4])
    start_fh, wait_fh = halo_rows(
        fp.at[pl.ds(3, 3)], fp.at[pl.ds(own, 3)], fp.at[pl.ds(0, 3)], fp.at[pl.ds(own + 3, 3)], fh_send, fh_recv
    )
    start_gh, wait_gh = halo_rows(
        gub.at[pl.ds(0, 3)], gub.at[pl.ds(own - 3, 3)], low.at[pl.ds(0, 3)], low.at[pl.ds(3, 3)], gh_send, gh_recv
    )
    start_r, wait_r = give_rows(own, result, result_out, r_send, r_recv, stay.at[5])
    start_g, wait_g = give_rows(own, gf, gf_out, g_send, g_recv, stay.at[6])

    def widen(src, at, rows, dst, to):
        dst[to : to + rows] = src[at : at + rows].astype(f32).reshape((rows, circle, channels))

    greet(sizes)
    start_f()
    for load in loads:
        load.wait()
    wait_f()
    start_fh()
    start_c()
    widen(fp, 3, own, pad, 3)
    convolve(pad, weight, update, own, False, False)
    wait_fh()
    widen(fp, 0, 3, pad, 0)
    widen(fp, own + 3, 3, pad, own + 3)
    convolve(pad, weight, update, own, False, True)
    steps = core_step(
        cr, update, gain_ref[...], wq, wo, result, gpad.at[pl.ds(3, own)], gub, bigs[2:], bigs[0], gg
    )
    next(steps)
    start_r()
    wait_c()
    next(steps)
    head[0]()
    next(steps)
    start_gh()
    next(steps)
    for stream in body:
        stream[0]()
    head[1]()
    next(steps)
    correlate_rows(pad, gpad.at[pl.ds(3, own)], conv, own, 0, 2)
    for stream in body:
        stream[1]()
    correlate_rows(pad, gpad.at[pl.ds(3, own)], conv, own, 2, channels // LANES)
    pack_small(bigs[1], conv, gg)
    small[0]()
    head[2]()
    convolve(gpad, weight, out, own, True, False)
    small[1]()
    for stream in body:
        stream[2]()
    head[3]()
    wait_gh()
    widen(low, 0, 3, gpad, 0)
    widen(low, 3, 3, gpad, own + 3)
    convolve(gpad, weight, out, own, True, True)
    gf[...] = out[...].reshape(gf.shape).astype(bf16)
    start_g()
    for k in range(2, len(small)):
        small[k]()
        if k + 1 < len(small):
            for stream in body:
                stream[k + 1]()
        if k + 2 < len(small):
            head[k + 2]()
    sent_f()
    sent_c()
    wait_r()
    wait_g()


STREAMS = 5


def on_device(sizes, fields, cotangent, conv_weight, norm_gain, w_qkv, w_out):
    n_lat, n_lon, n_dp = sizes
    batch, rows, cols, channels = fields.shape
    own, circle = rows // n_lon, cols * n_lon
    att = w_out.shape[0]
    bf16, f32 = jnp.bfloat16, jnp.float32
    shape = jax.ShapeDtypeStruct
    sems = pltpu.SemaphoreType.DMA
    vmem = pltpu.VMEM
    third = w_qkv.shape[1] // 3
    pieces = [(att // 4, channels), (16, channels)] + [(channels // 4, third)] * 3
    blocked = (own, n_lon, cols, channels)
    flat = (own, circle, channels)
    padded = (own + 6, circle, channels)
    sums = []
    for r, w in pieces:
        sums += [vmem((n, r, w), bf16) for n in (4, 2, 2)] + [vmem((r, w), bf16)] * 5
        sums += [sems((8,)), sems((8,))]
    inside = pl.BlockSpec(memory_space=pltpu.VMEM)
    outside = pl.BlockSpec(memory_space=pl.ANY)
    outs = pl.pallas_call(
        functools.partial(layer, sizes),
        out_shape=[shape((rows, cols, channels), bf16)] * 2 + [shape((4, r, w), bf16) for r, w in pieces],
        in_specs=[outside, outside, outside, inside, outside, outside],
        out_specs=[outside] * 2 + [inside] * STREAMS,
        scratch_shapes=[
            vmem((own + 6,) + blocked[1:], bf16), vmem(blocked, bf16), vmem(conv_weight.shape, f32),
            vmem(w_qkv.shape, bf16), vmem(w_out.shape, bf16),
            vmem(padded, f32), vmem(flat, f32), vmem(blocked, bf16), vmem(padded, f32), vmem(blocked, bf16),
            vmem((1, channels), f32), vmem((6,) + blocked[1:], bf16), vmem(flat, f32), vmem(blocked, bf16),
            vmem(conv_weight.shape, f32),
            sems((4,)), sems((4,)), sems((4,)), sems((4,)), sems((7,)), sems((2,)), sems((2,)), sems((2,)), sems((2,)),
            sems((4,)), sems((4,)), sems((4,)), sems((4,)),
        ] + sums,
        compiler_params=pltpu.CompilerParams(
            vmem_limit_bytes=67043328, collective_id=1, has_side_effects=True
        ),
    )(fields[0], cotangent[0], conv_weight, norm_gain.reshape(1, channels), w_qkv, w_out)
    outs = pl.pallas_call(
        finish,
        out_shape=[shape((rows, cols, channels), bf16)] * 2
        + [shape(w_qkv.shape, f32), shape(w_out.shape, f32), shape(conv_weight.shape, f32),
           shape((1, channels), f32)],
        in_specs=[inside] * len(outs),
        out_specs=[inside] * 6,
        compiler_params=pltpu.CompilerParams(vmem_limit_bytes=67043328),
    )(*outs)
    return outs[0][None], outs[1][None], outs[2], outs[3], outs[4], outs[5].reshape(channels)


def pick(mesh, *args):
    sizes = tuple(mesh.shape[a] for a in AXES)
    _, rows, cols, channels = args[0].shape
    att = args[5].shape[0]
    n_lat, n_lon, n_dp = sizes
    fits = (
        args[0].shape[0] == 1 and n_lat == 2 and n_dp == 2 and n_lon == 4
        and rows % n_lon == 0 and rows // n_lon >= 3 and cols % 8 == 0
        and LANES % (cols * n_lon) == 0 and (rows // n_lon * cols * n_lon) % LANES == 0
        and args[2].shape[:2] == (7, 7) and channels % LANES == 0 and att % LANES == 0
        and args[4].shape[1] == 3 * att
    )
    return on_device(sizes, *args) if fits else on_device_native(*args)


def solution(mesh):
    placed = (
        P(("member", "dp"), "lat", "lon", None),
        P(("member", "dp"), "lat", "lon", None),
        P(),
        P(),
        P(),
        P(),
    )
    return jax.shard_map(
        functools.partial(pick, mesh),
        mesh=mesh,
        in_specs=placed,
        out_specs=(
            P(("member", "dp"), "lat", "lon", None),
            P(("member", "dp"), "lat", "lon", None),
            P("member", None),
            P("member", None),
            P("member", None, None),
            P("member"),
        ),
        check_vma=False,
    )
```

```python
import functools
import itertools

import jax
import jax.numpy as jnp
from jax import lax
from jax.experimental import pallas as pl
from jax.experimental.pallas import tpu as pltpu
from jax.sharding import PartitionSpec as P

HEADS = 4
HEAD_DIM = 64


EPSILON = 1e-06


def with_halo(x, sides, width, wrap):
    for axis, dim in sides:
        size, length = (lax.axis_size(axis), x.shape[dim])
        up = [(i, (i + 1) % size) for i in range(size if wrap else size - 1)]
        down = [(j, i) for i, j in up]
        last = lax.slice_in_dim(x, length - width, length, axis=dim)
        first = lax.slice_in_dim(x, 0, width, axis=dim)
        before = lax.ppermute(last, axis, up)
        after = lax.ppermute(first, axis, down)
        x = jnp.concatenate([before, x, after], axis=dim)
    return x


def spread(padded, kernel, lat_rows, lon_cols):
    summed = jnp.zeros(padded.shape[:1] + (lat_rows, lon_cols, padded.shape[3]), jnp.float32)
    for row_shift in range(7):
        band = padded[:, row_shift : row_shift + lat_rows].astype(jnp.float32)
        partial_row = kernel[row_shift, 0] * band[:, :, 0:lon_cols]
        for col_shift in range(1, 7):
            partial_row = (
                partial_row
                + kernel[row_shift, col_shift] * band[:, :, col_shift : col_shift + lon_cols]
            )
        summed = summed + partial_row
    return summed


def correlate(padded, upstream, lat_rows, lon_cols):
    pieces = []
    for row_shift in range(7):
        for col_shift in range(7):
            window = padded[
                :, row_shift : row_shift + lat_rows, col_shift : col_shift + lon_cols
            ].astype(jnp.float32)
            pieces.append(jnp.sum(window * upstream, axis=(0, 1, 2)))
    return jnp.stack(pieces).reshape(7, 7, -1)


def split_heads(values):
    return values.reshape(values.shape[:-1] + (HEADS, HEAD_DIM))


def attend_forward(rowwise, att_width):
    queries = split_heads(rowwise[..., :att_width])
    keys_part = split_heads(rowwise[..., att_width : 2 * att_width])
    values_part = split_heads(rowwise[..., 2 * att_width :])
    scores = jnp.einsum(
        "brqhd,brkhd->brhqk", queries, keys_part, preferred_element_type=jnp.float32
    ) * HEAD_DIM ** (-0.5)
    row_peak = jnp.max(scores, -1, keepdims=True)
    raised = jnp.exp(scores - row_peak)
    probs = raised / jnp.sum(raised, -1, keepdims=True)
    weights = probs.astype(jnp.bfloat16)
    mixed = jnp.einsum(
        "brhqk,brkhd->brqhd", weights, values_part, preferred_element_type=jnp.float32
    )
    return (mixed.reshape(rowwise.shape[:3] + (att_width,)).astype(jnp.bfloat16), probs)


def attend_backward(rowwise, probs, grad_rowwise, att_width):
    queries = split_heads(rowwise[..., :att_width])
    keys_part = split_heads(rowwise[..., att_width : 2 * att_width])
    values_part = split_heads(rowwise[..., 2 * att_width :])
    grad_heads = split_heads(grad_rowwise)
    weights = probs.astype(jnp.bfloat16)
    grad_probs = jnp.einsum(
        "brqhd,brkhd->brhqk", grad_heads, values_part, preferred_element_type=jnp.float32
    )
    inner = jnp.sum(probs * grad_probs, -1, keepdims=True)
    grad_scores = (probs * (grad_probs - inner) * HEAD_DIM ** (-0.5)).astype(jnp.bfloat16)
    grad_query = jnp.einsum(
        "brhqk,brkhd->brqhd", grad_scores, keys_part, preferred_element_type=jnp.float32
    )
    grad_key = jnp.einsum(
        "brhqk,brqhd->brkhd", grad_scores, queries, preferred_element_type=jnp.float32
    )
    grad_value = jnp.einsum(
        "brhqk,brqhd->brkhd", weights, grad_heads, preferred_element_type=jnp.float32
    )
    shaped = rowwise.shape[:3] + (att_width,)
    return jnp.concatenate(
        [
            grad_query.reshape(shaped).astype(jnp.bfloat16),
            grad_key.reshape(shaped).astype(jnp.bfloat16),
            grad_value.reshape(shaped).astype(jnp.bfloat16),
        ],
        axis=-1,
    )


def contract_rows(left, right):
    return lax.dot_general(
        left, right, (((0,), (0,)), ((), ())), preferred_element_type=jnp.float32
    )


def contract_cols(left, right):
    return lax.dot_general(
        left, right, (((1,), (1,)), ((), ())), preferred_element_type=jnp.float32
    )


def on_device_native(fields, cotangent, conv_weight, norm_gain, w_qkv, w_out):
    batch_count, lat_rows, lon_cols, channels = fields.shape
    att_width = w_out.shape[0]
    wide = with_halo(fields, (("lon", 2),), 3, True)
    padded = with_halo(wide, (("lat", 1),), 3, False)
    update = fields.astype(jnp.float32) + spread(padded, conv_weight, lat_rows, lon_cols)
    inverse = lax.rsqrt(jnp.mean(update * update, -1, keepdims=True) + EPSILON)
    normed = (update * inverse * norm_gain).astype(jnp.bfloat16)
    normed_flat = normed.reshape(-1, channels)
    projected = jnp.dot(normed_flat, w_qkv, preferred_element_type=jnp.float32).astype(jnp.bfloat16)
    rowwise = lax.all_to_all(
        projected.reshape(batch_count, lat_rows, lon_cols, 3 * att_width),
        "lon",
        split_axis=1,
        concat_axis=2,
        tiled=True,
    )
    mixed_rows, probs = attend_forward(rowwise, att_width)
    mixed = lax.all_to_all(mixed_rows, "lon", split_axis=2, concat_axis=1, tiled=True)
    mixed_flat = mixed.reshape(-1, att_width)
    result = (
        update
        + jnp.dot(mixed_flat, w_out, preferred_element_type=jnp.float32).reshape(update.shape)
    ).astype(jnp.bfloat16)
    upstream_flat = cotangent.reshape(-1, channels)
    grad_mixed = contract_cols(upstream_flat, w_out).astype(jnp.bfloat16)
    grad_out = contract_rows(mixed_flat, upstream_flat)
    grad_rowwise = lax.all_to_all(
        grad_mixed.reshape(batch_count, lat_rows, lon_cols, att_width),
        "lon",
        split_axis=1,
        concat_axis=2,
        tiled=True,
    )
    grad_projected_rows = attend_backward(rowwise, probs, grad_rowwise, att_width)
    grad_projected = lax.all_to_all(
        grad_projected_rows, "lon", split_axis=2, concat_axis=1, tiled=True
    )
    grad_flat = grad_projected.reshape(-1, 3 * att_width)
    grad_weight = contract_rows(normed_flat, grad_flat)
    grad_normed = contract_cols(grad_flat, w_qkv).reshape(update.shape)
    grad_gain = jnp.sum(grad_normed * (update * inverse), axis=(0, 1, 2))
    gained = norm_gain * grad_normed
    grad_update = (
        cotangent.astype(jnp.float32)
        + inverse * gained
        - update * inverse**3 * jnp.mean(gained * update, -1, keepdims=True)
    )
    grad_wide = with_halo(grad_update.astype(jnp.bfloat16), (("lon", 2),), 3, True).astype(
        grad_update.dtype
    )
    grad_padded = with_halo(grad_wide.astype(jnp.bfloat16), (("lat", 1),), 3, False).astype(
        grad_wide.dtype
    )
    grad_fields = (
        grad_update + spread(grad_padded, conv_weight[::-1, ::-1], lat_rows, lon_cols)
    ).astype(jnp.bfloat16)
    grad_conv = correlate(padded, grad_update, lat_rows, lon_cols)
    totals = lax.psum((grad_weight, grad_out, grad_conv, grad_gain), ("lon", "lat", "dp"))
    return (result, grad_fields, totals[0], totals[1], totals[2], totals[3])


MESH = pl.DeviceIdType.MESH
AXES = ("lat", "lon", "dp")
LANES = 128


def place():
    return tuple(lax.axis_index(a) for a in AXES)


def greet(sizes):
    me = place()
    barrier = pltpu.get_barrier_semaphore()
    count = 0
    for offset in itertools.product(*(range(s) for s in sizes)):
        if not any(offset) or (offset[0] and any(offset[1:])):
            continue
        target = {a: lax.rem(m + o, s) for a, m, o, s in zip(AXES, me, offset, sizes)}
        pl.semaphore_signal(barrier, inc=1, device_id=target, device_id_type=MESH)
        count += 1
    pl.semaphore_wait(barrier, count)


def remote(src, dst, send, recv, target):
    return pltpu.make_async_remote_copy(
        src_ref=src, dst_ref=dst, send_sem=send, recv_sem=recv, device_id=target, device_id_type=MESH
    )


def roles(own, low, count):
    lat, lon, dp = place()
    side = lon // 2
    spot = 2 * lax.rem(lon, 2) + dp

    def block(p):
        return p + lat * (3 - 2 * p)

    def owner(p):
        return {"lon": 2 * dp + p // 2, "dp": p % 2}

    def mine(p):
        return (lon == 2 * dp + p // 2) & (dp == p % 2)

    def source(i):
        return {"lon": i, "dp": side}

    def local(i):
        return (lon == i) & (dp == side)

    def rows(p):
        return pl.ds(own * block(p) + low, count)

    return lon, spot, owner, mine, source, local, rows


def take_rows(own, src, dst, send, recv, stay):
    lon, _, owner, mine, source, local, rows = roles(own, 0, own)

    def there(p):
        return remote(src.at[rows(p)], dst.at[:, lon], send.at[p], recv.at[lon], owner(p))

    def here(p, i):
        return pltpu.make_async_copy(src.at[rows(p)], dst.at[:, i], stay)

    def start():
        for p in range(4):

            @pl.when(jnp.logical_not(mine(p)))
            def _(p=p):
                there(p).start()

            @pl.when(mine(p))
            def _(p=p):
                here(p, lon).start()

    def wait():
        for i in range(4):

            @pl.when(local(i))
            def _(i=i):
                here(0, i).wait()

            @pl.when(jnp.logical_not(local(i)))
            def _(i=i):
                remote(src.at[rows(0)], dst.at[:, i], send.at[0], recv.at[i], source(i)).wait_recv()

    def wait_sent():
        for p in range(4):

            @pl.when(jnp.logical_not(mine(p)))
            def _(p=p):
                there(p).wait_send()

    return start, wait, wait_sent


def give_rows(own, low, count, src, dst, send, recv, stay):
    lon, spot, owner, mine, source, local, rows = roles(own, low, count)
    part = src.at[pl.ds(low, count)]

    def there(i):
        return remote(part.at[:, i], dst.at[rows(spot)], send.at[i], recv.at[spot], source(i))

    def here(i):
        return pltpu.make_async_copy(part.at[:, i], dst.at[rows(spot)], stay)

    def start():
        for i in range(4):

            @pl.when(jnp.logical_not(local(i)))
            def _(i=i):
                there(i).start()

            @pl.when(local(i))
            def _(i=i):
                here(i).start()

    def wait():
        for p in range(4):

            @pl.when(jnp.logical_not(mine(p)))
            def _(p=p):
                remote(part.at[:, 0], dst.at[rows(p)], send.at[0], recv.at[p], owner(p)).wait_recv()

        for i in range(4):

            @pl.when(jnp.logical_not(local(i)))
            def _(i=i):
                there(i).wait_send()

            @pl.when(local(i))
            def _(i=i):
                here(i).wait()

    return start, wait


def halo_rows(first, last, top, low, send, recv):
    lat, lon, dp = place()
    side = lon // 2
    spot = 2 * lax.rem(lon, 2) + dp
    index, end = 4 * lat + spot + lat * (3 - 2 * spot), 7

    def at(k):
        k = lax.rem(k + 8, 8)
        band = k // 4
        b = lax.rem(k, 4)
        p = b + band * (3 - 2 * b)
        return {"lat": band, "lon": 2 * side + p // 2, "dp": lax.rem(p, 2)}

    down = remote(last, top, send.at[0], recv.at[0], at(index + 1))
    up = remote(first, low, send.at[1], recv.at[1], at(index + 7))

    def start():
        @pl.when(index < end)
        def _():
            down.start()

        @pl.when(index > 0)
        def _():
            up.start()

        @pl.when(index == 0)
        def _():
            top[...] = jnp.zeros(top.shape, top.dtype)

        @pl.when(index == end)
        def _():
            low[...] = jnp.zeros(low.shape, low.dtype)

    def wait():
        @pl.when(index > 0)
        def _():
            down.wait_recv()
            up.wait_send()

        @pl.when(index < end)
        def _():
            up.wait_recv()
            down.wait_send()

    return start, wait


def convolve(pad, weight, out, own, flip, halo):
    circle, channels = pad.shape[1], pad.shape[2]
    taken = {}
    for r in range(own):
        taps = [a for a in range(7) if (3 <= r + a < own + 3) != halo]
        if taps:
            taken[r] = taps

    def chunk(c, carry):
        lanes = pl.ds(pl.multiple_of(c * LANES, LANES), LANES)
        totals = {r: out[r, :, lanes] if halo else pad[r + 3, :, lanes] for r in taken}
        for e in range(7):
            turn = (3 - e) % circle
            column = 6 - e if flip else e
            taps = [weight[6 - a if flip else a, column : column + 1, lanes] for a in range(7)]
            for r in taken:
                part = None
                for a in taken[r]:
                    term = pad[r + a, :, lanes] * taps[a]
                    part = term if part is None else part + term
                if turn:
                    part = pltpu.roll(part, turn, 0)
                totals[r] = totals[r] + part
        for r in taken:
            out[r, :, lanes] = totals[r]
        return carry

    lax.fori_loop(0, channels // LANES, chunk, 0)


def correlate_rows(pad, upstream, out, own, low, high):
    circle = pad.shape[1]

    def chunk(c, carry):
        lanes = pl.ds(pl.multiple_of(c * LANES, LANES), LANES)
        for e in range(7):
            turn = (e - 3) % circle
            turned = [upstream[r, :, lanes] for r in range(own)]
            if turn:
                turned = [pltpu.roll(t, turn, 0) for t in turned]
            for a in range(7):
                total = None
                for r in range(own):
                    term = pad[r + a, :, lanes] * turned[r]
                    total = term if total is None else total + term
                out[a, e : e + 1, lanes] = jnp.sum(total, axis=0, keepdims=True)
        return carry

    lax.fori_loop(low, high, chunk, 0)


def dot(left, right, dims):
    return lax.dot_general(left, right, (dims, ((), ())), preferred_element_type=jnp.float32)


PLAIN, COLS, ROWS = ((1,), (0,)), ((1,), (1,)), ((0,), (0,))


def attend_rows(projected, circle, att_width):
    cells = projected.shape[0]
    group = max(circle, LANES)
    row_of = lax.broadcasted_iota(jnp.int32, (group, group), 0) // circle
    col_of = lax.broadcasted_iota(jnp.int32, (group, group), 1) // circle
    same = row_of == col_of
    lane_head = lax.broadcasted_iota(jnp.int32, (group, LANES), 1) // HEAD_DIM
    bf16 = jnp.bfloat16
    zero = jnp.zeros((), bf16)
    heads = range(LANES // HEAD_DIM)
    groups = [slice(g * group, (g + 1) * group) for g in range(cells // group)]
    pairs = [slice(p * LANES, (p + 1) * LANES) for p in range(att_width // LANES)]

    def third(k, cut, at):
        return projected[cut, k * att_width : (k + 1) * att_width][:, at]

    def join(parts):
        whole = parts[0]
        for h in heads[1:]:
            whole = jnp.where(lane_head == h, parts[h], whole)
        return whole.astype(bf16)

    kept, mixed = {}, []
    for g, cut in enumerate(groups):
        found = []
        for p, at in enumerate(pairs):
            q, k, v = (third(n, cut, at) for n in range(3))
            parts = []
            for h in heads:
                scores = dot(jnp.where(lane_head == h, q, zero), k, COLS) * HEAD_DIM ** (-0.5)
                scores = jnp.where(same, scores, -jnp.inf)
                raised = jnp.exp(scores - jnp.max(scores, -1, keepdims=True))
                probs = raised / jnp.sum(raised, -1, keepdims=True)
                kept[g, p, h] = probs
                parts.append(dot(probs.astype(bf16), v, PLAIN))
            found.append(join(parts))
        mixed.append(jnp.concatenate(found, axis=1))

    def backward(grad_mixed):
        grads = []
        for g, cut in enumerate(groups):
            found = [[], [], []]
            for p, at in enumerate(pairs):
                q, k, v = (third(n, cut, at) for n in range(3))
                up = grad_mixed[cut, at]
                parts = [[], [], []]
                for h in heads:
                    probs = kept[g, p, h]
                    grad_probs = dot(jnp.where(lane_head == h, up, zero), v, COLS)
                    inner = jnp.sum(probs * grad_probs, -1, keepdims=True)
                    grad_scores = (probs * (grad_probs - inner) * HEAD_DIM ** (-0.5)).astype(bf16)
                    parts[0].append(dot(grad_scores, k, PLAIN))
                    parts[1].append(dot(grad_scores, q, ROWS))
                    parts[2].append(dot(probs.astype(bf16), up, ROWS))
                for part, into in zip(parts, found):
                    into.append(join(part))
            grads.append(jnp.concatenate(found[0] + found[1] + found[2], axis=1))
        return jnp.concatenate(grads, axis=0)

    return jnp.concatenate(mixed, axis=0), backward


def core_step(cr_ref, update_ref, gain, wq_ref, wo_ref, result_ref, gu_ref, gub_ref, bq_refs, bo_ref, gg_ref):
    own, blocks, width, channels = cr_ref.shape
    circle, cells = blocks * width, own * blocks * width
    att_width = wo_ref.shape[0]
    bf16 = jnp.bfloat16
    update = update_ref[...].reshape(cells, channels)
    inverse = lax.rsqrt(jnp.mean(update * update, -1, keepdims=True) + EPSILON)
    normed = (update * inverse * gain).astype(bf16)
    projected = dot(normed, wq_ref[...], PLAIN).astype(bf16)
    mixed, backward = attend_rows(projected, circle, att_width)
    result = update + dot(mixed, wo_ref[...], PLAIN)
    result_ref[...] = result.reshape(result_ref.shape).astype(bf16)
    yield
    cot32 = cr_ref[...].astype(jnp.float32).reshape(cells, channels)
    cot = cot32.astype(bf16)
    bo_ref[...] = dot(mixed, cot, ROWS).astype(bf16).reshape(bo_ref.shape)
    yield
    grad_mixed = dot(cot, wo_ref[...], COLS).astype(bf16)
    grad_projected = backward(grad_mixed)
    for k, ref in enumerate(bq_refs):
        part = ref.shape[2]
        piece = dot(normed, grad_projected[:, k * part : (k + 1) * part], ROWS)
        ref[...] = piece.astype(bf16).reshape(ref.shape)
    yield
    grad_normed = dot(grad_projected, wq_ref[...], COLS)
    gained = gain * grad_normed
    grad_update = (
        cot32
        + inverse * gained
        - update * (inverse * inverse * inverse) * jnp.mean(gained * update, -1, keepdims=True)
    )
    gu_ref[...] = grad_update.reshape(gu_ref.shape)
    gub_ref[...] = grad_update.reshape(gub_ref.shape).astype(bf16)
    yield
    gg_ref[...] = jnp.sum(grad_normed * (update * inverse), axis=0, keepdims=True)
    yield


def pack_small(big, conv, gg_ref):
    channels = gg_ref.shape[1]
    fill = big.shape[0] * big.shape[1] - 50
    small = jnp.concatenate(
        [conv[a] for a in range(7)] + [gg_ref[...], jnp.zeros((fill, channels), jnp.float32)], axis=0
    )
    big[...] = small.astype(jnp.bfloat16).reshape(big.shape)


def finish(*refs):
    every, outs = refs[: len(refs) - 6], refs[len(refs) - 6 :]
    result_ref, gf_ref, out_ref, small_ref = every[:4]
    result_out, gf_out, gq_out, go_out, gc_out, gg_out = outs
    f32 = jnp.float32
    result_out[...] = result_ref[...]
    gf_out[...] = gf_ref[...]
    for k, ref in enumerate(every[4:]):
        part = ref.shape[2]
        gq_out[:, k * part : (k + 1) * part] = ref[...].astype(f32).reshape(gq_out.shape[0], part)
    go_out[...] = out_ref[...].astype(f32).reshape(go_out.shape)
    small = small_ref[...].astype(f32).reshape(-1, go_out.shape[1])
    for a in range(7):
        gc_out[a] = small[a * 7 : (a + 1) * 7]
    gg_out[...] = small[49:50]


def sum_stages(big, every, got1, sum1, got2, sum2, got3, sum3, got4, send, recv):
    lat, lon, dp = place()
    f32 = jnp.float32
    other_dp, other_lat = 1 - dp, 1 - lat
    half = lon // 2
    inner = (lon == 1) | (lon == 2)
    outer = jnp.logical_not(inner)
    mine, across = every.at[2 * dp + lat], every.at[2 * dp + other_lat]
    core = remote(big.at[pl.ds(2 * other_dp, 2)], got1, send.at[0], recv.at[0], {"dp": other_dp})
    band = remote(sum1.at[other_lat], got2, send.at[1], recv.at[1], {"lat": other_lat})
    inward = remote(sum2, got3, send.at[2], recv.at[2], {"lon": 1 + half})
    middle = remote(sum3, got4, send.at[3], recv.at[3], {"lon": 3 - lon})
    outward = remote(mine, mine, send.at[4], recv.at[4], {"lon": 3 * half})
    out_band = remote(mine, mine, send.at[5], recv.at[5], {"lat": other_lat})
    in_band = remote(across, across, send.at[5], recv.at[5], {"lat": other_lat})
    ours, theirs = every.at[pl.ds(2 * dp, 2)], every.at[pl.ds(2 * other_dp, 2)]
    out_core = remote(ours, ours, send.at[6], recv.at[6], {"dp": other_dp})
    in_core = remote(theirs, theirs, send.at[6], recv.at[6], {"dp": other_dp})

    def add(a, b, to):
        to[...] = (a[...].astype(f32) + b[...].astype(f32)).astype(to.dtype)

    def s0():
        core.start()

    def s1():
        core.wait()
        add(big.at[pl.ds(2 * dp, 2)], got1, sum1)
        band.start()

    def s2():
        band.wait()
        add(sum1.at[lat], got2, sum2)

        @pl.when(outer)
        def _():
            inward.start()

    def s3():
        @pl.when(inner)
        def _():
            inward.wait_recv()
            add(sum2, got3, sum3)
            middle.start()

    def s4():
        @pl.when(inner)
        def _():
            middle.wait()
            add(sum3, got4, mine)
            outward.start()
            out_band.start()

    def s5():
        @pl.when(outer)
        def _():
            outward.wait_recv()
            out_band.start()

    def s6():
        in_band.wait_recv()
        out_core.start()

    def s7():
        out_core.wait_send()
        in_core.wait_recv()
        out_band.wait_send()

        @pl.when(inner)
        def _():
            outward.wait_send()

        @pl.when(outer)
        def _():
            inward.wait_send()

    return s0, s1, s2, s3, s4, s5, s6, s7


def sum_stages_near(big, every, got1, sum1, got2, sum2, got3, sum3, got4, send, recv):
    lat, lon, dp = place()
    f32 = jnp.float32
    other_dp, other_lat = 1 - dp, 1 - lat
    near, far = lon + 1 - 2 * lax.rem(lon, 2), lax.rem(lon + 2, 4)
    mine, across = every.at[2 * dp + lat], every.at[2 * dp + other_lat]
    core = remote(big.at[pl.ds(2 * other_dp, 2)], got1, send.at[0], recv.at[0], {"dp": other_dp})
    band = remote(sum1.at[other_lat], got2, send.at[1], recv.at[1], {"lat": other_lat})
    one = remote(sum2, got3, send.at[2], recv.at[2], {"lon": near})
    two = remote(sum3, got4, send.at[3], recv.at[3], {"lon": far})
    out_band = remote(mine, mine, send.at[4], recv.at[4], {"lat": other_lat})
    in_band = remote(across, across, send.at[4], recv.at[4], {"lat": other_lat})
    ours, theirs = every.at[pl.ds(2 * dp, 2)], every.at[pl.ds(2 * other_dp, 2)]
    out_core = remote(ours, ours, send.at[5], recv.at[5], {"dp": other_dp})
    in_core = remote(theirs, theirs, send.at[5], recv.at[5], {"dp": other_dp})

    def add(a, b, to):
        to[...] = (a[...].astype(f32) + b[...].astype(f32)).astype(to.dtype)

    def s0():
        core.start()

    def s1():
        core.wait_recv()
        add(big.at[pl.ds(2 * dp, 2)], got1, sum1)
        band.start()

    def s2():
        band.wait_recv()
        add(sum1.at[lat], got2, sum2)
        one.start()

    def s3():
        one.wait_recv()
        add(sum2, got3, sum3)
        two.start()

    def s4():
        two.wait_recv()
        add(sum3, got4, mine)
        out_band.start()

    def s5():
        in_band.wait_recv()
        out_core.start()

    def s6():
        in_core.wait_recv()
        for copy in (core, band, one, two, out_band, out_core):
            copy.wait_send()

    return s0, s1, s2, s3, s4, s5, s6


def layer(sizes, f_ref, c_ref, w_hbm, gain_ref, wq_hbm, wo_hbm, result_out, gf_out, *rest):
    every, rest = rest[:STREAMS], rest[STREAMS:]
    (fp, cr, weight, wq, wo, pad, update, result, gpad, gub, gg, low, out, gf, conv,
     f_send, f_recv, c_send, c_recv, stay, fh_send, fh_recv, gh_send, gh_recv,
     r_send, r_recv, g_send, g_recv), rest = rest[:28], rest[28:]
    own, circle, channels = update.shape
    f32, bf16 = jnp.float32, jnp.bfloat16
    loads = [
        pltpu.make_async_copy(src, dst, stay.at[k])
        for k, (src, dst) in enumerate(((w_hbm, weight), (wq_hbm, wq), (wo_hbm, wo)))
    ]
    for load in loads:
        load.start()
    per = len(rest) // STREAMS
    bigs = [rest[k * per] for k in range(STREAMS)]
    streams = []
    for k in range(STREAMS):
        refs = rest[k * per : (k + 1) * per]
        streams.append((sum_stages_near if k == 1 else sum_stages)(refs[0], every[k], *refs[1:]))
    head, small, body = streams[0], streams[1], streams[2:]
    start_f, wait_f, sent_f = take_rows(own, f_ref, fp.at[pl.ds(3, own)], f_send, f_recv, stay.at[3])
    start_c, wait_c, sent_c = take_rows(own, c_ref, cr, c_send, c_recv, stay.at[4])
    start_fh, wait_fh = halo_rows(
        fp.at[pl.ds(3, 3)], fp.at[pl.ds(own, 3)], fp.at[pl.ds(0, 3)], fp.at[pl.ds(own + 3, 3)], fh_send, fh_recv
    )
    start_gh, wait_gh = halo_rows(
        gub.at[pl.ds(0, 3)], gub.at[pl.ds(own - 3, 3)], low.at[pl.ds(0, 3)], low.at[pl.ds(3, 3)], gh_send, gh_recv
    )
    cut = own // 2
    returns = []
    for src, dst, send, recv, at in ((result, result_out, r_send, r_recv, 5), (gf, gf_out, g_send, g_recv, 7)):
        for k, (low_row, count) in enumerate(((0, cut), (cut, own - cut))):
            returns.append(give_rows(own, low_row, count, src, dst, send.at[k], recv.at[k], stay.at[at + k]))
    def widen(src, at, rows, dst, to):
        dst[to : to + rows] = src[at : at + rows].astype(f32).reshape((rows, circle, channels))

    greet(sizes)
    start_f()
    for load in loads:
        load.wait()
    wait_f()
    start_fh()
    start_c()
    widen(fp, 3, own, pad, 3)
    convolve(pad, weight, update, own, False, False)
    wait_fh()
    widen(fp, 0, 3, pad, 0)
    widen(fp, own + 3, 3, pad, own + 3)
    convolve(pad, weight, update, own, False, True)
    steps = core_step(
        cr, update, gain_ref[...], wq, wo, result, gpad.at[pl.ds(3, own)], gub, bigs[2:], bigs[0], gg
    )
    next(steps)
    returns[0][0]()
    wait_c()
    next(steps)
    head[0]()
    next(steps)
    for stream in body:
        stream[0]()
    head[1]()
    next(steps)
    start_gh()
    returns[1][0]()
    for stream in body:
        stream[1]()
    next(steps)
    correlate_rows(pad, gpad.at[pl.ds(3, own)], conv, own, 0, channels // LANES)
    pack_small(bigs[1], conv, gg)
    small[0]()
    head[2]()
    convolve(gpad, weight, out, own, True, False)
    small[1]()
    for stream in body:
        stream[2]()
    head[3]()
    wait_gh()
    widen(low, 0, 3, gpad, 0)
    widen(low, 3, 3, gpad, own + 3)
    convolve(gpad, weight, out, own, True, True)
    gf[...] = out[...].reshape(gf.shape).astype(bf16)
    for k in range(3, 8):
        small[k - 1]()
        for stream in body:
            stream[k]()
        if k + 1 < 8:
            head[k + 1]()
        if k == 4:
            returns[2][0]()
        if k == 4:
            returns[3][0]()
    sent_f()
    sent_c()
    for _, wait in returns:
        wait()


STREAMS = 8


def on_device(sizes, fields, cotangent, conv_weight, norm_gain, w_qkv, w_out):
    n_lat, n_lon, n_dp = sizes
    batch, rows, cols, channels = fields.shape
    own, circle = rows // n_lon, cols * n_lon
    att = w_out.shape[0]
    bf16, f32 = jnp.bfloat16, jnp.float32
    shape = jax.ShapeDtypeStruct
    sems = pltpu.SemaphoreType.DMA
    vmem = pltpu.VMEM
    width = w_qkv.shape[1] // (STREAMS - 2)
    pieces = [(att // 4, channels), (16, channels)] + [(channels // 4, width)] * (STREAMS - 2)
    blocked = (own, n_lon, cols, channels)
    flat = (own, circle, channels)
    padded = (own + 6, circle, channels)
    sums = []
    for r, w in pieces:
        sums += [vmem((n, r, w), bf16) for n in (4, 2, 2)] + [vmem((r, w), bf16)] * 5
        sums += [sems((8,)), sems((8,))]
    inside = pl.BlockSpec(memory_space=pltpu.VMEM)
    outside = pl.BlockSpec(memory_space=pl.ANY)
    outs = pl.pallas_call(
        functools.partial(layer, sizes),
        out_shape=[shape((rows, cols, channels), bf16)] * 2 + [shape((4, r, w), bf16) for r, w in pieces],
        in_specs=[outside, outside, outside, inside, outside, outside],
        out_specs=[outside] * 2 + [inside] * STREAMS,
        scratch_shapes=[
            vmem((own + 6,) + blocked[1:], bf16), vmem(blocked, bf16), vmem(conv_weight.shape, f32),
            vmem(w_qkv.shape, bf16), vmem(w_out.shape, bf16),
            vmem(padded, f32), vmem(flat, f32), vmem(blocked, bf16), vmem(padded, f32), vmem(blocked, bf16),
            vmem((1, channels), f32), vmem((6,) + blocked[1:], bf16), vmem(flat, f32), vmem(blocked, bf16),
            vmem(conv_weight.shape, f32),
            sems((4,)), sems((4,)), sems((4,)), sems((4,)), sems((9,)), sems((2,)), sems((2,)), sems((2,)), sems((2,)),
            sems((2, 4)), sems((2, 4)), sems((2, 4)), sems((2, 4)),
        ] + sums,
        compiler_params=pltpu.CompilerParams(
            vmem_limit_bytes=67043328, collective_id=1, has_side_effects=True
        ),
    )(fields[0], cotangent[0], conv_weight, norm_gain.reshape(1, channels), w_qkv, w_out)
    outs = pl.pallas_call(
        finish,
        out_shape=[shape((rows, cols, channels), bf16)] * 2
        + [shape(w_qkv.shape, f32), shape(w_out.shape, f32), shape(conv_weight.shape, f32),
           shape((1, channels), f32)],
        in_specs=[inside] * len(outs),
        out_specs=[inside] * 6,
        compiler_params=pltpu.CompilerParams(vmem_limit_bytes=67043328),
    )(*outs)
    return outs[0][None], outs[1][None], outs[2], outs[3], outs[4], outs[5].reshape(channels)


def pick(mesh, *args):
    sizes = tuple(mesh.shape[a] for a in AXES)
    _, rows, cols, channels = args[0].shape
    att = args[5].shape[0]
    n_lat, n_lon, n_dp = sizes
    fits = (
        args[0].shape[0] == 1 and n_lat == 2 and n_dp == 2 and n_lon == 4
        and rows % n_lon == 0 and rows // n_lon >= 3 and cols % 8 == 0
        and LANES % (cols * n_lon) == 0 and (rows // n_lon * cols * n_lon) % LANES == 0
        and args[2].shape[:2] == (7, 7) and channels % LANES == 0 and att % LANES == 0
        and args[4].shape[1] == 3 * att and 3 * att % ((STREAMS - 2) * LANES) == 0
    )
    return on_device(sizes, *args) if fits else on_device_native(*args)


def solution(mesh):
    placed = (
        P(("member", "dp"), "lat", "lon", None),
        P(("member", "dp"), "lat", "lon", None),
        P(),
        P(),
        P(),
        P(),
    )
    return jax.shard_map(
        functools.partial(pick, mesh),
        mesh=mesh,
        in_specs=placed,
        out_specs=(
            P(("member", "dp"), "lat", "lon", None),
            P(("member", "dp"), "lat", "lon", None),
            P("member", None),
            P("member", None),
            P("member", None, None),
            P("member"),
        ),
        check_vma=False,
    )
```
